128 devices in a mesh: grp: 4 (over y), mem: 32 (over x, z, core).
Axes of the slice: x: 4, y: 4, z: 4, core: 2. Of those that a mesh axis runs over, the one named last changes fastest.
Arguments:
- features: bfloat16 [524288, 1024], P(('grp', 'mem')), may hold values from -24 to 24
- lengths: int32 [128, 2], P(('grp', 'mem')), may hold values from 512 to 2048, as said below
Outputs:
- sample_count: float32 [1], replicated
- feature_mean: float32 [1024], replicated
- covariance: float32 [1024, 1024], P(('grp', 'mem'))
The draws below stay inside these ranges and needn't reach their ends.
Inputs may be any that keep to these rules, and one draw needn't show every extreme that they name: Every block of a device has 2048 slots; lengths count the valid leading slots.
All inputs are finite; a program needn't handle non-finite values.
Results may differ from the reference program's by a relative error of at most 0.0003.
Values sent between devices are 32-bit elements; how exact they have to be, the bound alone decides.
A program may use at most 64 MiB of HBM per device.

```python
import jax
import jax.numpy as jnp
from jax import lax

D = 1024
BLOCK_ROWS = 2048
SHARDS = 128
IMAGES = 524288


def draw_features(key, part):
    key_scale = jax.random.fold_in(key, 11)
    key_offset = jax.random.fold_in(key, 12)
    key_noise = jax.random.fold_in(key, 13)
    scales = 0.3 * jnp.exp(jax.random.uniform(key_scale, (D,), jnp.float32, 0.0, jnp.log(10.0)))
    offsets = jnp.clip(jax.random.normal(key_offset, (D,), jnp.float32), -3.0, 3.0)
    noise = jnp.clip(jax.random.normal(key_noise, (IMAGES, D), jnp.float32), -6.0, 6.0)
    return (noise * scales[None, :] + offsets[None, :]).astype(jnp.bfloat16)


def draw_lengths(key, part):
    index = jnp.arange(SHARDS, dtype=jnp.int32)
    upper = BLOCK_ROWS // 4 + 1 + 3 * BLOCK_ROWS // 4 * (index + 1) // SHARDS
    values = jax.random.randint(key, (SHARDS, 2), BLOCK_ROWS // 4, upper[:, None])
    values = values.at[0, 0].set(BLOCK_ROWS // 4)
    values = values.at[SHARDS - 1, 1].set(BLOCK_ROWS)
    return values.astype(jnp.int32)


def setup_inputs(seed: int = 0) -> dict:
    seeds = jax.random.split(jax.random.key(seed), 3)
    features = draw_features(jax.random.fold_in(seeds[2], 71), 0)
    lengths = draw_lengths(jax.random.fold_in(seeds[2], 71), 0)
    return {"features": features, "lengths": lengths}


def reference(features, lengths):
    total = jnp.sum(lengths).astype(jnp.float32)
    blocks = features.reshape(SHARDS * 2, BLOCK_ROWS, D)
    position = jnp.arange(BLOCK_ROWS, dtype=jnp.int32)
    weights = (position[None, :] < lengths.reshape(SHARDS * 2, 1)).astype(jnp.float32)

    def add_sum(acc, item):
        block, mask = item
        return acc + jnp.sum(block.astype(jnp.float32) * mask[:, None], axis=0), None

    sums, _ = lax.scan(add_sum, jnp.zeros((D,), jnp.float32), (blocks, weights))
    feature_mean = sums / total

    def add_gram(acc, item):
        block, mask = item
        centred = (block.astype(jnp.float32) - feature_mean[None, :]) * mask[:, None]
        return acc + jnp.dot(centred.T, centred, precision=lax.Precision.HIGHEST), None

    second, _ = lax.scan(add_gram, jnp.zeros((D, D), jnp.float32), (blocks, weights))
    covariance = second / (total - 1.0)
    return total.reshape(1), feature_mean, covariance
```

```python
import functools

import jax
import jax.numpy as jnp
from jax import lax
from jax.experimental import pallas as pl
from jax.experimental.pallas import tpu as pltpu
from jax.sharding import PartitionSpec as P

MESH = pl.DeviceIdType.MESH
ROWS = 4096
HALF = 2048
D = 1024
BLK = 256
LOADS = 4
KLOAD = ROWS // LOADS
UNITS = 8
ORDERS = ("yxz", "xzy", "zyx")


def kernel(
    len_ref, feat, stats_ref, cov_ref,
    xb, dacc, grid, p1, p2, p3, rc, r1, r2, r3,
    s0, sc, sx, sy, sz,
    lsem, csend, crecv, gsend, grecv, asend, arecv,
):
    y = lax.axis_index("grp")
    m = lax.axis_index("mem")
    x, z, c = m // 8, (m // 2) % 4, m % 2
    pos = {"y": y, "x": x, "z": z}

    def device(axis, d):
        at = dict(pos)
        at[axis] = (pos[axis] + d) % 4
        return (at["y"], at["x"] * 8 + at["z"] * 2 + c)

    partner = (y, x * 8 + z * 2 + (1 - c))

    def load(k):
        rows = pl.ds(pl.multiple_of(k * KLOAD, KLOAD), KLOAD)
        return pltpu.make_async_copy(feat.at[rows], xb.at[rows], lsem.at[k])

    for k in range(LOADS):
        load(k).start()

    barrier = pltpu.get_barrier_semaphore()
    pl.semaphore_signal(barrier, inc=1, device_id=partner, device_id_type=MESH)
    for axis in "xyz":
        for d in (1, 2, 3):
            pl.semaphore_signal(barrier, inc=1, device_id=device(axis, d), device_id_type=MESH)

    s0[0] = jnp.zeros((8, 128), jnp.float32)

    def first(k, sums):
        load(k).wait()
        rows = pl.ds(pl.multiple_of(k * KLOAD, KLOAD), KLOAD)
        length = len_ref[0, k // 2]
        at = lax.broadcasted_iota(jnp.int32, (KLOAD, 128), 0) + (k % 2) * KLOAD
        keep = (at < length).astype(jnp.float32).astype(jnp.bfloat16)
        out = []
        for t in range(8):
            part = xb[rows, 128 * t:128 * t + 128] * keep
            xb[rows, 128 * t:128 * t + 128] = part
            out.append(
                sums[t] + part.astype(jnp.float32).reshape(KLOAD // 8, 8, 128).sum(axis=0)
            )
        prod = lax.dot_general(
            xb[rows, 0:BLK], xb[rows, :], (((0,), (0,)), ((), ())),
            preferred_element_type=jnp.float32,
        )

        @pl.when(k == 0)
        def _():
            dacc[...] = prod

        @pl.when(k > 0)
        def _():
            dacc[...] += prod

        return tuple(out)

    sums = lax.fori_loop(
        0, LOADS, first, tuple(jnp.zeros((8, 128), jnp.float32) for _ in range(8))
    )
    for t in range(8):
        s0[0, t:t + 1, :] = jnp.sum(sums[t], axis=0, keepdims=True)
    s0[1] = jnp.full((8, 128), (len_ref[0, 0] + len_ref[0, 1]).astype(jnp.float32))

    def place(j):
        for i in range(j, 4):
            for h in range(2):
                col = BLK * (i - j) + 128 * h
                grid[2 * i + h, 16 * j:16 * j + 16] = dacc[:, col:col + 128].reshape(16, 2, 8, 128)
            if i > j:
                turned = dacc[:, BLK * (i - j):BLK * (i - j) + BLK].T
                for h in range(2):
                    grid[2 * j + h, 16 * i:16 * i + 16] = (
                        turned[:, 128 * h:128 * h + 128].reshape(16, 2, 8, 128)
                    )

    def product(j, half):
        rows = pl.ds(half * HALF, HALF)
        return lax.dot_general(
            xb[rows, BLK * j:BLK * j + BLK], xb[rows, BLK * j:], (((0,), (0,)), ((), ())),
            preferred_element_type=jnp.float32,
        )

    def pair_copy(u):
        return pltpu.make_async_remote_copy(
            src_ref=grid.at[u, :, 1 - c], dst_ref=rc.at[u],
            send_sem=csend.at[u], recv_sem=crecv.at[u],
            device_id=partner, device_id_type=MESH,
        )

    def axis_copy(u, stage, d):
        order = ORDERS[u % 3]
        axis = order[stage]
        to = (pos[axis] + d) % 4
        if stage == 0:
            src = {"y": p1.at[u, to], "x": p1.at[u, :, to], "z": p1.at[u, :, :, to]}[axis]
            dst = r1.at[u, d - 1]
        elif stage == 1:
            src = p2.at[u, :, to] if order == "xzy" else p2.at[u, to]
            dst = r2.at[u, d - 1]
        else:
            src = p3.at[u, to]
            dst = r3.at[u, d - 1]
        return pltpu.make_async_remote_copy(
            src_ref=src, dst_ref=dst,
            send_sem=gsend.at[u, stage, d - 1], recv_sem=grecv.at[u, stage, d - 1],
            device_id=device(axis, d), device_id_type=MESH,
        )

    def send_pair(u):
        pair_copy(u).start()

    def step(u, stage):
        order = ORDERS[u % 3]
        if stage == 0:
            pair_copy(u).wait_recv()
            p1[u] = grid[u, :, c].reshape(4, 4, 4, 8, 128) + rc[u].reshape(4, 4, 4, 8, 128)
        else:
            for d in (1, 2, 3):
                axis_copy(u, stage - 1, d).wait_recv()
            at = pos[order[stage - 1]]
            if stage == 1:
                own = {"y": lambda: p1[u, at], "x": lambda: p1[u, :, at], "z": lambda: p1[u, :, :, at]}[order[0]]()
                p2[u] = (own + r1[u, 0]) + (r1[u, 1] + r1[u, 2])
            elif stage == 2:
                own = p2[u, :, at] if order == "xzy" else p2[u, at]
                p3[u] = (own + r2[u, 0]) + (r2[u, 1] + r2[u, 2])
        for d in (1, 2, 3):
            axis_copy(u, stage, d).start()

    def sum_pair():
        return pltpu.make_async_remote_copy(
            src_ref=s0, dst_ref=sc, send_sem=asend.at[9], recv_sem=arecv.at[9],
            device_id=partner, device_id_type=MESH,
        )

    stages = (("x", sx), ("y", sy), ("z", sz))

    def sum_copy(i, d):
        axis, buf = stages[i]
        return pltpu.make_async_remote_copy(
            src_ref=buf.at[pos[axis]], dst_ref=buf.at[pos[axis]],
            send_sem=asend.at[3 * i + d - 1], recv_sem=arecv.at[3 * i + d - 1],
            device_id=device(axis, d), device_id_type=MESH,
        )

    def sum_step(i):
        if i == 0:
            sum_pair().wait_recv()
            value = s0[...] + sc[...]
        else:
            for d in (1, 2, 3):
                sum_copy(i - 1, d).wait_recv()
            buf = stages[i - 1][1]
            value = (buf[0] + buf[1]) + (buf[2] + buf[3])
        if i < 3:
            axis, buf = stages[i]
            buf[pos[axis]] = value
            for d in (1, 2, 3):
                sum_copy(i, d).start()
        return value

    pl.semaphore_wait(barrier, 10)
    sum_pair().start()
    place(0)
    send_pair(0)
    send_pair(1)

    dacc[:, 0:768] = product(1, 0)
    sum_step(0)
    step(0, 0)
    step(1, 0)
    dacc[:, 0:768] += product(1, 1)
    place(1)
    send_pair(2)
    send_pair(3)
    dacc[:, 0:512] = product(2, 0)
    step(2, 0)
    step(3, 0)
    dacc[:, 0:512] += product(2, 1)
    place(2)
    send_pair(4)
    send_pair(5)
    dacc[:, 0:256] = product(3, 0)
    step(4, 0)
    step(5, 0)
    dacc[:, 0:256] += product(3, 1)
    place(3)
    send_pair(6)
    send_pair(7)

    sum_step(1)
    step(0, 1)
    step(1, 1)
    step(6, 0)
    step(7, 0)
    step(2, 1)
    step(3, 1)
    sum_step(2)
    step(0, 2)
    step(1, 2)
    step(4, 1)
    step(5, 1)
    step(2, 2)
    step(3, 2)
    step(6, 1)
    step(7, 1)
    total = sum_step(3)
    step(4, 2)
    step(5, 2)
    step(6, 2)
    step(7, 2)

    count = total[1]
    mean = total[0] / count
    stats_ref[0] = mean
    stats_ref[1] = count
    index = y * 32 + m
    row = stats_ref[0, pl.ds(index // 16, 1), :]
    lane = lax.broadcasted_iota(jnp.int32, (8, 128), 1)
    sub = lax.broadcasted_iota(jnp.int32, (8, 128), 0)
    picked = jnp.where(lane == (index % 16) * 8 + sub, jnp.broadcast_to(row, (8, 128)), 0.0)
    own_mean = jnp.sum(picked, axis=1, keepdims=True)
    scale = 1.0 / (count - 1.0)
    for u in range(UNITS):
        for d in (1, 2, 3):
            axis_copy(u, 2, d).wait_recv()
        at = pos[ORDERS[u % 3][2]]
        second = (p3[u, at] + r3[u, 0]) + (r3[u, 1] + r3[u, 2])
        outer = own_mean * stats_ref[0, u:u + 1, :]
        cov_ref[:, 128 * u:128 * u + 128] = (second - count * outer) / (count - 1.0)

    sum_pair().wait_send()
    for i in range(3):
        for d in (1, 2, 3):
            sum_copy(i, d).wait_send()
    for u in range(UNITS):
        pair_copy(u).wait_send()
        for stage in range(3):
            for d in (1, 2, 3):
                axis_copy(u, stage, d).wait_send()


def body(features, lengths):
    f32 = jnp.float32
    stats, cov = pl.pallas_call(
        kernel,
        out_shape=(
            jax.ShapeDtypeStruct((2, 8, 128), f32),
            jax.ShapeDtypeStruct((8, D), f32),
        ),
        in_specs=[
            pl.BlockSpec(memory_space=pltpu.SMEM),
            pl.BlockSpec(memory_space=pl.ANY),
        ],
        out_specs=(
            pl.BlockSpec(memory_space=pltpu.VMEM),
            pl.BlockSpec(memory_space=pltpu.VMEM),
        ),
        scratch_shapes=[
            pltpu.VMEM((ROWS, D), jnp.bfloat16),
            pltpu.VMEM((BLK, D), f32),
            pltpu.VMEM((UNITS, 64, 2, 8, 128), f32),
            pltpu.VMEM((UNITS, 4, 4, 4, 8, 128), f32),
            pltpu.VMEM((UNITS, 4, 4, 8, 128), f32),
            pltpu.VMEM((UNITS, 4, 8, 128), f32),
            pltpu.VMEM((UNITS, 64, 8, 128), f32),
            pltpu.VMEM((UNITS, 3, 4, 4, 8, 128), f32),
            pltpu.VMEM((UNITS, 3, 4, 8, 128), f32),
            pltpu.VMEM((UNITS, 3, 8, 128), f32),
            pltpu.VMEM((2, 8, 128), f32),
            pltpu.VMEM((2, 8, 128), f32),
            pltpu.VMEM((4, 2, 8, 128), f32),
            pltpu.VMEM((4, 2, 8, 128), f32),
            pltpu.VMEM((4, 2, 8, 128), f32),
            pltpu.SemaphoreType.DMA((LOADS,)),
            pltpu.SemaphoreType.DMA((UNITS,)),
            pltpu.SemaphoreType.DMA((UNITS,)),
            pltpu.SemaphoreType.DMA((UNITS, 3, 3)),
            pltpu.SemaphoreType.DMA((UNITS, 3, 3)),
            pltpu.SemaphoreType.DMA((10,)),
            pltpu.SemaphoreType.DMA((10,)),
        ],
        compiler_params=pltpu.CompilerParams(
            collective_id=0, has_side_effects=True, vmem_limit_bytes=60 * 1024 * 1024
        ),
        name="gram_reduce",
    )(lengths, features)
    return stats[1, 0, 0:1], stats[0].reshape(D), cov


def solution(mesh):
    return jax.shard_map(
        body,
        mesh=mesh,
        in_specs=(P(("grp", "mem"), None), P(("grp", "mem"), None)),
        out_specs=(P(), P(), P(("grp", "mem"), None)),
        check_vma=False,
    )
```

```python
import functools

import jax
import jax.numpy as jnp
from jax import lax
from jax.experimental import pallas as pl
from jax.experimental.pallas import tpu as pltpu
from jax.sharding import PartitionSpec as P

MESH = pl.DeviceIdType.MESH
ROWS = 4096
D = 1024
BLK = 128
LOADS = 4
KLOAD = ROWS // LOADS
UNITS = 8
ORDERS = ("yxz", "xzy", "zyx")


def kernel(
    len_hbm, feat, stats_ref, cov_ref,
    len_ref, xb, kt, da, db, grid, p1, p2, p3, rc, r1, r2, r3,
    s0, sc, sx, sy, sz,
    nsem, lsem, csend, crecv, gsend, grecv, asend, arecv,
):
    y = lax.axis_index("grp")
    m = lax.axis_index("mem")
    x, z, c = m // 8, (m // 2) % 4, m % 2
    pos = {"y": y, "x": x, "z": z}

    def device(axis, d):
        at = dict(pos)
        at[axis] = (pos[axis] + d) % 4
        return (at["y"], at["x"] * 8 + at["z"] * 2 + c)

    partner = (y, x * 8 + z * 2 + (1 - c))

    def load(k):
        rows = pl.ds(pl.multiple_of(k * KLOAD, KLOAD), KLOAD)
        return pltpu.make_async_copy(feat.at[rows], xb.at[rows], lsem.at[k])

    lengths_copy = pltpu.make_async_copy(len_hbm, len_ref, nsem.at[0])
    lengths_copy.start()
    for k in range(LOADS):
        load(k).start()

    barrier = pltpu.get_barrier_semaphore()
    pl.semaphore_signal(barrier, inc=1, device_id=partner, device_id_type=MESH)
    for axis in "xyz":
        for d in (1, 2, 3):
            pl.semaphore_signal(barrier, inc=1, device_id=device(axis, d), device_id_type=MESH)

    da[...] = jnp.zeros(da.shape, jnp.float32)
    lengths_copy.wait()

    def first(k, carry):
        load(k).wait()
        rows = pl.ds(pl.multiple_of(k * KLOAD, KLOAD), KLOAD)
        at = lax.broadcasted_iota(jnp.int32, (16, KLOAD), 1) + (k % 2) * KLOAD
        keep = (at < len_ref[0, k // 2]).astype(jnp.float32).astype(jnp.bfloat16)
        kt[:, rows] = keep
        left = xb[rows, 0:BLK].T * jnp.concatenate([keep] * 8, axis=0)
        da[...] += jnp.dot(
            jnp.concatenate([left, keep], axis=0), xb[rows, :],
            preferred_element_type=jnp.float32,
        )
        return carry

    lax.fori_loop(0, LOADS, first, 0)
    for t in range(8):
        s0[0, t:t + 1, :] = da[BLK:BLK + 1, 128 * t:128 * t + 128]
    s0[1] = jnp.full((8, 128), (len_ref[0, 0] + len_ref[0, 1]).astype(jnp.float32))

    def put(u, i, value):
        value = value.reshape(2, 4, 2, 8, 128)
        at = 2 * (i % 2)
        for core in range(2):
            grid[u, core, i // 2, at:at + 2] = value[:, :, core]

    def place(j, dacc):
        for i in range(j, UNITS):
            part = dacc[0:BLK, BLK * (i - j):BLK * (i - j) + BLK]
            put(i, j, part)
            if i > j:
                put(j, i, part.T)

    def product(j, dacc):
        left = xb[:, BLK * j:BLK * j + BLK].T * jnp.concatenate([kt[...]] * 8, axis=0)
        dacc[0:BLK, 0:D - BLK * j] = jnp.dot(
            left, xb[:, BLK * j:], preferred_element_type=jnp.float32
        )

    def pair_copy(u):
        return pltpu.make_async_remote_copy(
            src_ref=grid.at[u, 1 - c], dst_ref=rc.at[u],
            send_sem=csend.at[u], recv_sem=crecv.at[u],
            device_id=partner, device_id_type=MESH,
        )

    def axis_copy(u, stage, d):
        axis = ORDERS[u % 3][stage]
        to = (pos[axis] + d) % 4
        src = (p1, p2, p3)[stage].at[u, to]
        dst = (r1, r2, r3)[stage].at[u, d - 1]
        return pltpu.make_async_remote_copy(
            src_ref=src, dst_ref=dst,
            send_sem=gsend.at[u, stage, d - 1], recv_sem=grecv.at[u, stage, d - 1],
            device_id=device(axis, d), device_id_type=MESH,
        )

    def send_pair(u):
        pair_copy(u).start()

    def gather(u, stage):
        order = ORDERS[u % 3]
        if stage == 0:
            pair_copy(u).wait_recv()
            if order == "yxz":
                p1[u] = grid[u, c] + rc[u]
            else:
                for i in range(4):
                    for k in range(4):
                        if order == "xzy":
                            p1[u, i, k] = grid[u, c, :, i, k] + rc[u, :, i, k]
                        else:
                            p1[u, i, k] = grid[u, c, k, :, i] + rc[u, k, :, i]
        else:
            for d in (1, 2, 3):
                axis_copy(u, stage - 1, d).wait_recv()
            src, got, dst = ((p1, r1, p2), (p2, r2, p3))[stage - 1]
            own = src[u, pos[order[stage - 1]]]
            dst[u] = (own + got[u, 0]) + (got[u, 1] + got[u, 2])

    def step(units, stage):
        for u in units:
            gather(u, stage)
        for d in (2, 1, 3):
            for u in units:
                axis_copy(u, stage, d).start()

    def sum_pair():
        return pltpu.make_async_remote_copy(
            src_ref=s0, dst_ref=sc, send_sem=asend.at[9], recv_sem=arecv.at[9],
            device_id=partner, device_id_type=MESH,
        )

    stages = (("x", sx), ("y", sy), ("z", sz))

    def sum_copy(i, d):
        axis, buf = stages[i]
        return pltpu.make_async_remote_copy(
            src_ref=buf.at[pos[axis]], dst_ref=buf.at[pos[axis]],
            send_sem=asend.at[3 * i + d - 1], recv_sem=arecv.at[3 * i + d - 1],
            device_id=device(axis, d), device_id_type=MESH,
        )

    def sum_step(i):
        if i == 0:
            sum_pair().wait_recv()
            value = s0[...] + sc[...]
        else:
            for d in (1, 2, 3):
                sum_copy(i - 1, d).wait_recv()
            buf = stages[i - 1][1]
            value = (buf[0] + buf[1]) + (buf[2] + buf[3])
        if i < 3:
            axis, buf = stages[i]
            buf[pos[axis]] = value
            for d in (1, 2, 3):
                sum_copy(i, d).start()
        return value

    pl.semaphore_wait(barrier, 10)
    sum_pair().start()

    place(0, da)
    send_pair(0)
    for j in range(1, UNITS):
        buf = (da, db)[j % 2]
        product(j, buf)
        place(j, buf)
        send_pair(j)
        if j == 1:
            sum_step(0)
            step((0,), 0)
        if j == 2:
            step((1,), 0)
    early, middle, late = (0, 1), (2, 3, 4), (5, 6, 7)
    step(middle, 0)
    step(late, 0)
    sum_step(1)
    step(early, 1)
    step(middle, 1)
    sum_step(2)
    step(early, 2)
    step(late, 1)
    step(middle, 2)
    total = sum_step(3)
    step(late, 2)

    count = total[1]
    mean = total[0] / count
    stats_ref[0] = mean
    stats_ref[1] = count
    index = y * 32 + m
    row = stats_ref[0, pl.ds(index // 16, 1), :]
    lane = lax.broadcasted_iota(jnp.int32, (8, 128), 1)
    sub = lax.broadcasted_iota(jnp.int32, (8, 128), 0)
    picked = jnp.where(lane == (index % 16) * 8 + sub, jnp.broadcast_to(row, (8, 128)), 0.0)
    own_mean = jnp.sum(picked, axis=1, keepdims=True)
    scale = 1.0 / (count - 1.0)
    for u in range(UNITS):
        for d in (1, 2, 3):
            axis_copy(u, 2, d).wait_recv()
        at = pos[ORDERS[u % 3][2]]
        second = (p3[u, at] + r3[u, 0]) + (r3[u, 1] + r3[u, 2])
        outer = own_mean * stats_ref[0, u:u + 1, :]
        cov_ref[:, 128 * u:128 * u + 128] = (second - count * outer) / (count - 1.0)

    sum_pair().wait_send()
    for i in range(3):
        for d in (1, 2, 3):
            sum_copy(i, d).wait_send()
    for u in range(UNITS):
        pair_copy(u).wait_send()
        for stage in range(3):
            for d in (1, 2, 3):
                axis_copy(u, stage, d).wait_send()


def finish(stats_ref, cov_ref, count_out, mean_out, cov_out):
    count_out[...] = stats_ref[1, 0:1, 0:1]
    mean_out[...] = stats_ref[0]
    cov_out[...] = cov_ref[...]


def body(features, lengths):
    f32 = jnp.float32
    stats, cov = pl.pallas_call(
        kernel,
        out_shape=(
            jax.ShapeDtypeStruct((2, 8, 128), f32),
            jax.ShapeDtypeStruct((8, D), f32),
        ),
        in_specs=[
            pl.BlockSpec(memory_space=pl.ANY),
            pl.BlockSpec(memory_space=pl.ANY),
        ],
        out_specs=(
            pl.BlockSpec(memory_space=pltpu.VMEM),
            pl.BlockSpec(memory_space=pltpu.VMEM),
        ),
        scratch_shapes=[
            pltpu.SMEM((1, 2), jnp.int32),
            pltpu.VMEM((ROWS, D), jnp.bfloat16),
            pltpu.VMEM((16, ROWS), jnp.bfloat16),
            pltpu.VMEM((BLK + 16, D), f32),
            pltpu.VMEM((BLK, D - BLK), f32),
            pltpu.VMEM((UNITS, 2, 4, 4, 4, 8, 128), f32),
            pltpu.VMEM((UNITS, 4, 4, 4, 8, 128), f32),
            pltpu.VMEM((UNITS, 4, 4, 8, 128), f32),
            pltpu.VMEM((UNITS, 4, 8, 128), f32),
            pltpu.VMEM((UNITS, 4, 4, 4, 8, 128), f32),
            pltpu.VMEM((UNITS, 3, 4, 4, 8, 128), f32),
            pltpu.VMEM((UNITS, 3, 4, 8, 128), f32),
            pltpu.VMEM((UNITS, 3, 8, 128), f32),
            pltpu.VMEM((2, 8, 128), f32),
            pltpu.VMEM((2, 8, 128), f32),
            pltpu.VMEM((4, 2, 8, 128), f32),
            pltpu.VMEM((4, 2, 8, 128), f32),
            pltpu.VMEM((4, 2, 8, 128), f32),
            pltpu.SemaphoreType.DMA((1,)),
            pltpu.SemaphoreType.DMA((LOADS,)),
            pltpu.SemaphoreType.DMA((UNITS,)),
            pltpu.SemaphoreType.DMA((UNITS,)),
            pltpu.SemaphoreType.DMA((UNITS, 3, 3)),
            pltpu.SemaphoreType.DMA((UNITS, 3, 3)),
            pltpu.SemaphoreType.DMA((10,)),
            pltpu.SemaphoreType.DMA((10,)),
        ],
        compiler_params=pltpu.CompilerParams(
            collective_id=0, has_side_effects=True, vmem_limit_bytes=63 * 1024 * 1024
        ),
        name="gram_reduce",
    )(lengths, features)
    count, mean, cov = pl.pallas_call(
        finish,
        out_shape=(
            jax.ShapeDtypeStruct((1, 1), f32),
            jax.ShapeDtypeStruct((8, 128), f32),
            jax.ShapeDtypeStruct((8, D), f32),
        ),
        in_specs=[pl.BlockSpec(memory_space=pltpu.VMEM)] * 2,
        out_specs=(pl.BlockSpec(memory_space=pltpu.VMEM),) * 3,
        name="finish",
    )(stats, cov)
    return count.reshape(1), mean.reshape(D), cov


def solution(mesh):
    return jax.shard_map(
        body,
        mesh=mesh,
        in_specs=(P(("grp", "mem"), None), P(("grp", "mem"), None)),
        out_specs=(P(), P(), P(("grp", "mem"), None)),
        check_vma=False,
    )
```

```python
import functools

import jax
import jax.numpy as jnp
from jax import lax
from jax.experimental import pallas as pl
from jax.experimental.pallas import tpu as pltpu
from jax.sharding import PartitionSpec as P

MESH = pl.DeviceIdType.MESH
ROWS = 4096
D = 1024
BLK = 128
LOADS = 4
KLOAD = ROWS // LOADS
UNITS = 8
ORDERS = ("yxz", "xzy", "zyx")


def order_of(f, u):
    return u % 3 if f == 3 else f


def kernel(
    len_hbm, feat, stats_ref, cov_ref,
    len_ref, xb, kt, da, db, grid, p1, p2, p3, rc, r1, r2, r3,
    s0, sc, sx, sy, sz,
    nsem, lsem, csend, crecv, gsend, grecv, asend, arecv,
):
    y = lax.axis_index("grp")
    m = lax.axis_index("mem")
    x, z, c = m // 8, (m // 2) % 4, m % 2
    pos = {"y": y, "x": x, "z": z}

    def device(axis, d):
        at = dict(pos)
        at[axis] = (pos[axis] + d) % 4
        return (at["y"], at["x"] * 8 + at["z"] * 2 + c)

    partner = (y, x * 8 + z * 2 + (1 - c))

    def load(k):
        rows = pl.ds(pl.multiple_of(k * KLOAD, KLOAD), KLOAD)
        return pltpu.make_async_copy(feat.at[rows], xb.at[rows], lsem.at[k])

    lengths_copy = pltpu.make_async_copy(len_hbm, len_ref, nsem.at[0])
    lengths_copy.start()
    for k in range(LOADS):
        load(k).start()

    barrier = pltpu.get_barrier_semaphore()
    pl.semaphore_signal(barrier, inc=1, device_id=partner, device_id_type=MESH)
    for axis in "xyz":
        for d in (1, 2, 3):
            pl.semaphore_signal(barrier, inc=1, device_id=device(axis, d), device_id_type=MESH)

    da[...] = jnp.zeros(da.shape, jnp.float32)
    lengths_copy.wait()

    def first(k, carry):
        load(k).wait()
        rows = pl.ds(pl.multiple_of(k * KLOAD, KLOAD), KLOAD)
        at = lax.broadcasted_iota(jnp.int32, (16, KLOAD), 1) + (k % 2) * KLOAD
        keep = (at < len_ref[0, k // 2]).astype(jnp.float32).astype(jnp.bfloat16)
        kt[:, rows] = keep
        left = xb[rows, 0:BLK].T * jnp.concatenate([keep] * 8, axis=0)
        da[...] += jnp.dot(
            jnp.concatenate([left, keep], axis=0), xb[rows, :],
            preferred_element_type=jnp.float32,
        )
        return carry

    lax.fori_loop(0, LOADS, first, 0)
    for t in range(8):
        s0[0, t:t + 1, :] = da[BLK:BLK + 1, 128 * t:128 * t + 128]
    s0[1] = jnp.full((8, 128), (len_ref[0, 0] + len_ref[0, 1]).astype(jnp.float32))

    def put(u, i, value):
        value = value.reshape(2, 4, 2, 8, 128)
        at = 2 * (i % 2)
        for core in range(2):
            grid[u, core, i // 2, at:at + 2] = value[:, :, core]

    def place(j, dacc):
        for i in range(j, UNITS):
            part = dacc[0:BLK, BLK * (i - j):BLK * (i - j) + BLK]
            put(i, j, part)
            if i > j:
                put(j, i, part.T)

    def product(j, dacc):
        left = xb[:, BLK * j:BLK * j + BLK].T * jnp.concatenate([kt[...]] * 8, axis=0)
        dacc[0:BLK, 0:D - BLK * j] = jnp.dot(
            left, xb[:, BLK * j:], preferred_element_type=jnp.float32
        )

    def pair_copy(u):
        return pltpu.make_async_remote_copy(
            src_ref=grid.at[u, 1 - c], dst_ref=rc.at[u],
            send_sem=csend.at[u], recv_sem=crecv.at[u],
            device_id=partner, device_id_type=MESH,
        )

    own_class = (x + y + z) % 4

    def axis_copy(u, f, stage, d):
        axis = ORDERS[order_of(f, u)][stage]
        to = (pos[axis] + d) % 4
        src = (p1, p2)[stage].at[u, f, to]
        dst = (r1, r2)[stage].at[u, f, d - 1]
        return pltpu.make_async_remote_copy(
            src_ref=src, dst_ref=dst,
            send_sem=gsend.at[u, stage], recv_sem=grecv.at[u, stage],
            device_id=device(axis, d), device_id_type=MESH,
        )

    def last_copy(u, d):
        f = (own_class + d) % 4
        o = jnp.where(f == 3, u % 3, f)
        ty = (y + jnp.where(o == 1, d, 0)) % 4
        tx = (x + jnp.where(o == 2, d, 0)) % 4
        tz = (z + jnp.where(o == 0, d, 0)) % 4
        return pltpu.make_async_remote_copy(
            src_ref=p3.at[u, f], dst_ref=r3.at[u, d - 1],
            send_sem=gsend.at[u, 2], recv_sem=grecv.at[u, 2],
            device_id=(ty, tx * 8 + tz * 2 + c), device_id_type=MESH,
        )

    def all_of(u, stage):
        buf = (r1, r2, r3)[stage].at[u]
        return pltpu.make_async_remote_copy(
            src_ref=buf, dst_ref=buf, send_sem=gsend.at[u, stage], recv_sem=grecv.at[u, stage],
            device_id=partner, device_id_type=MESH,
        )

    def send_pair(u):
        pair_copy(u).start()

    def step(u, stage):
        if stage == 0:
            pair_copy(u).wait_recv()
            for f in range(4):
                order = ORDERS[order_of(f, u)]
                for i in range(4):
                    for k in range(4):
                        at = {order[0]: i, order[1]: k, order[2]: (f - i - k) % 4}
                        where = (at["y"], at["x"], at["z"])
                        p1[u, f, i, k] = grid[(u, c) + where] + rc[(u,) + where]
        else:
            all_of(u, stage - 1).wait_recv()
            src, got, dst = ((p1, r1, p2), (p2, r2, p3))[stage - 1]
            for f in range(4):
                own = src[u, f, pos[ORDERS[order_of(f, u)][stage - 1]]]
                dst[u, f] = (own + got[u, f, 0]) + (got[u, f, 1] + got[u, f, 2])
        for d in (2, 1, 3):
            if stage == 2:
                last_copy(u, d).start()
            else:
                for f in range(4):
                    axis_copy(u, f, stage, d).start()

    def sum_pair():
        return pltpu.make_async_remote_copy(
            src_ref=s0, dst_ref=sc, send_sem=asend.at[9], recv_sem=arecv.at[9],
            device_id=partner, device_id_type=MESH,
        )

    stages = (("x", sx), ("y", sy), ("z", sz))

    def sum_copy(i, d):
        axis, buf = stages[i]
        return pltpu.make_async_remote_copy(
            src_ref=buf.at[pos[axis]], dst_ref=buf.at[pos[axis]],
            send_sem=asend.at[3 * i + d - 1], recv_sem=arecv.at[3 * i + d - 1],
            device_id=device(axis, d), device_id_type=MESH,
        )

    def sum_step(i):
        if i == 0:
            sum_pair().wait_recv()
            value = s0[...] + sc[...]
        else:
            for d in (1, 2, 3):
                sum_copy(i - 1, d).wait_recv()
            buf = stages[i - 1][1]
            value = (buf[0] + buf[1]) + (buf[2] + buf[3])
        if i < 3:
            axis, buf = stages[i]
            buf[pos[axis]] = value
            for d in (1, 2, 3):
                sum_copy(i, d).start()
        return value

    pl.semaphore_wait(barrier, 10)
    sum_pair().start()

    place(0, da)
    send_pair(0)
    for j in range(1, UNITS):
        buf = (da, db)[j % 2]
        product(j, buf)
        place(j, buf)
        if j < 6:
            send_pair(j)
        if j == 1:
            sum_step(0)
            step(0, 0)
        if j == 2:
            step(1, 0)
        if j == 3:
            step(2, 0)
        if j == 5:
            step(3, 0)
    send_pair(6)
    send_pair(7)
    for u, stage in (
        (4, 0), (5, 0), (0, 1), (6, 0), (7, 0), (-1, 1), (1, 1), (2, 1), (0, 2), (3, 1), (4, 1),
        (1, 2), (2, 2), (-1, 2), (5, 1), (6, 1), (7, 1), (3, 2), (4, 2), (5, 2), (6, 2), (7, 2),
    ):
        if u < 0:
            sum_step(stage)
        else:
            step(u, stage)
    total = sum_step(3)

    count = total[1]
    mean = total[0] / count
    stats_ref[0] = mean
    stats_ref[1] = count
    index = y * 32 + m
    row = stats_ref[0, pl.ds(index // 16, 1), :]
    lane = lax.broadcasted_iota(jnp.int32, (8, 128), 1)
    sub = lax.broadcasted_iota(jnp.int32, (8, 128), 0)
    picked = jnp.where(lane == (index % 16) * 8 + sub, jnp.broadcast_to(row, (8, 128)), 0.0)
    own_mean = jnp.sum(picked, axis=1, keepdims=True)
    scale = 1.0 / (count - 1.0)
    for u in range(UNITS):
        all_of(u, 2).wait_recv()
        second = (p3[u, own_class] + r3[u, 0]) + (r3[u, 1] + r3[u, 2])
        outer = own_mean * stats_ref[0, u:u + 1, :]
        cov_ref[:, 128 * u:128 * u + 128] = (second - count * outer) / (count - 1.0)

    sum_pair().wait_send()
    for i in range(3):
        for d in (1, 2, 3):
            sum_copy(i, d).wait_send()
    for u in range(UNITS):
        pair_copy(u).wait_send()
        for stage in range(3):
            all_of(u, stage).wait_send()


def finish(stats_ref, cov_ref, count_out, mean_out, cov_out):
    count_out[...] = stats_ref[1, 0:1, 0:1]
    mean_out[...] = stats_ref[0]
    cov_out[...] = cov_ref[...]


def body(features, lengths):
    f32 = jnp.float32
    stats, cov = pl.pallas_call(
        kernel,
        out_shape=(
            jax.ShapeDtypeStruct((2, 8, 128), f32),
            jax.ShapeDtypeStruct((8, D), f32),
        ),
        in_specs=[
            pl.BlockSpec(memory_space=pl.ANY),
            pl.BlockSpec(memory_space=pl.ANY),
        ],
        out_specs=(
            pl.BlockSpec(memory_space=pltpu.VMEM),
            pl.BlockSpec(memory_space=pltpu.VMEM),
        ),
        scratch_shapes=[
            pltpu.SMEM((1, 2), jnp.int32),
            pltpu.VMEM((ROWS, D), jnp.bfloat16),
            pltpu.VMEM((16, ROWS), jnp.bfloat16),
            pltpu.VMEM((BLK + 16, D), f32),
            pltpu.VMEM((BLK, D - BLK), f32),
            pltpu.VMEM((UNITS, 2, 4, 4, 4, 8, 128), f32),
            pltpu.VMEM((UNITS, 4, 4, 4, 8, 128), f32),
            pltpu.VMEM((UNITS, 4, 4, 8, 128), f32),
            pltpu.VMEM((UNITS, 4, 8, 128), f32),
            pltpu.VMEM((UNITS, 4, 4, 4, 8, 128), f32),
            pltpu.VMEM((UNITS, 4, 3, 4, 8, 128), f32),
            pltpu.VMEM((UNITS, 4, 3, 8, 128), f32),
            pltpu.VMEM((UNITS, 3, 8, 128), f32),
            pltpu.VMEM((2, 8, 128), f32),
            pltpu.VMEM((2, 8, 128), f32),
            pltpu.VMEM((4, 2, 8, 128), f32),
            pltpu.VMEM((4, 2, 8, 128), f32),
            pltpu.VMEM((4, 2, 8, 128), f32),
            pltpu.SemaphoreType.DMA((1,)),
            pltpu.SemaphoreType.DMA((LOADS,)),
            pltpu.SemaphoreType.DMA((UNITS,)),
            pltpu.SemaphoreType.DMA((UNITS,)),
            pltpu.SemaphoreType.DMA((UNITS, 3)),
            pltpu.SemaphoreType.DMA((UNITS, 3)),
            pltpu.SemaphoreType.DMA((10,)),
            pltpu.SemaphoreType.DMA((10,)),
        ],
        compiler_params=pltpu.CompilerParams(
            collective_id=0, has_side_effects=True, vmem_limit_bytes=63 * 1024 * 1024
        ),
        name="gram_reduce",
    )(lengths, features)
    count, mean, cov = pl.pallas_call(
        finish,
        out_shape=(
            jax.ShapeDtypeStruct((1, 1), f32),
            jax.ShapeDtypeStruct((8, 128), f32),
            jax.ShapeDtypeStruct((8, D), f32),
        ),
        in_specs=[pl.BlockSpec(memory_space=pltpu.VMEM)] * 2,
        out_specs=(pl.BlockSpec(memory_space=pltpu.VMEM),) * 3,
        name="finish",
    )(stats, cov)
    return count.reshape(1), mean.reshape(D), cov


def solution(mesh):
    return jax.shard_map(
        body,
        mesh=mesh,
        in_specs=(P(("grp", "mem"), None), P(("grp", "mem"), None)),
        out_specs=(P(), P(), P(("grp", "mem"), None)),
        check_vma=False,
    )
```

```python
import functools

import jax
import jax.numpy as jnp
from jax import lax
from jax.experimental import pallas as pl
from jax.experimental.pallas import tpu as pltpu
from jax.sharding import PartitionSpec as P

MESH = pl.DeviceIdType.MESH
ROWS = 4096
D = 1024
BLK = 128
PAIR = 256
LOADS = 4
KLOAD = ROWS // LOADS
UNITS = 8
ORDERS = ("yxz", "xzy", "zyx")


def order_of(f, u):
    return u % 3 if f == 3 else f


def kernel(
    len_hbm, feat, stats_ref, cov_ref,
    len_ref, xb, kt, da, db, grid, p1, p2, p3, rc, r1, r2, r3,
    s0, sc, sx, sy, sz,
    nsem, lsem, csend, crecv, gsend, grecv, asend, arecv,
):
    y = lax.axis_index("grp")
    m = lax.axis_index("mem")
    x, z, c = m // 8, (m // 2) % 4, m % 2
    pos = {"y": y, "x": x, "z": z}

    def device(axis, d):
        at = dict(pos)
        at[axis] = (pos[axis] + d) % 4
        return (at["y"], at["x"] * 8 + at["z"] * 2 + c)

    partner = (y, x * 8 + z * 2 + (1 - c))

    def load(k):
        rows = pl.ds(pl.multiple_of(k * KLOAD, KLOAD), KLOAD)
        return pltpu.make_async_copy(feat.at[rows], xb.at[rows], lsem.at[k])

    lengths_copy = pltpu.make_async_copy(len_hbm, len_ref, nsem.at[0])
    lengths_copy.start()
    for k in range(LOADS):
        load(k).start()

    barrier = pltpu.get_barrier_semaphore()
    pl.semaphore_signal(barrier, inc=1, device_id=partner, device_id_type=MESH)
    for axis in "xyz":
        for d in (1, 2, 3):
            pl.semaphore_signal(barrier, inc=1, device_id=device(axis, d), device_id_type=MESH)

    da[...] = jnp.zeros(da.shape, jnp.float32)
    lengths_copy.wait()

    def first(k, carry):
        load(k).wait()
        rows = pl.ds(pl.multiple_of(k * KLOAD, KLOAD), KLOAD)
        at = lax.broadcasted_iota(jnp.int32, (16, KLOAD), 1) + (k % 2) * KLOAD
        keep = (at < len_ref[0, k // 2]).astype(jnp.float32).astype(jnp.bfloat16)
        kt[:, rows] = keep
        left = xb[rows, 0:PAIR].T * jnp.concatenate([keep] * 16, axis=0)
        da[...] += jnp.dot(
            jnp.concatenate([left, keep], axis=0), xb[rows, :],
            preferred_element_type=jnp.float32,
        )
        return carry

    lax.fori_loop(0, LOADS, first, 0)
    for t in range(8):
        s0[0, t:t + 1, :] = da[PAIR:PAIR + 1, 128 * t:128 * t + 128]
    s0[1] = jnp.full((8, 128), (len_ref[0, 0] + len_ref[0, 1]).astype(jnp.float32))

    def put(u, i, value):
        value = value.reshape(2, 4, 2, 8, 128)
        at = 2 * (i % 2)
        for core in range(2):
            grid[u, core, i // 2, at:at + 2] = value[:, :, core]

    def place(p, dacc):
        for j in (2 * p, 2 * p + 1):
            row = BLK * (j - 2 * p)
            for i in range(j, UNITS):
                col = BLK * (i - 2 * p)
                part = dacc[row:row + BLK, col:col + BLK]
                put(i, j, part)
                if i > j:
                    put(j, i, part.T)

    def product(p, dacc):
        left = xb[:, PAIR * p:PAIR * p + PAIR].T * jnp.concatenate([kt[...]] * 16, axis=0)
        dacc[0:PAIR, 0:D - PAIR * p] = jnp.dot(
            left, xb[:, PAIR * p:], preferred_element_type=jnp.float32
        )

    def pair_copy(u):
        return pltpu.make_async_remote_copy(
            src_ref=grid.at[u, 1 - c], dst_ref=rc.at[u],
            send_sem=csend.at[u], recv_sem=crecv.at[u],
            device_id=partner, device_id_type=MESH,
        )

    own_class = (x + y + z) % 4

    def axis_copy(u, f, stage, d):
        axis = ORDERS[order_of(f, u)][stage]
        to = (pos[axis] + d) % 4
        src = (p1, p2)[stage].at[u, f, to]
        dst = (r1, r2)[stage].at[u, f, d - 1]
        return pltpu.make_async_remote_copy(
            src_ref=src, dst_ref=dst,
            send_sem=gsend.at[u, stage], recv_sem=grecv.at[u, stage],
            device_id=device(axis, d), device_id_type=MESH,
        )

    def last_copy(u, d):
        f = (own_class + d) % 4
        o = jnp.where(f == 3, u % 3, f)
        ty = (y + jnp.where(o == 1, d, 0)) % 4
        tx = (x + jnp.where(o == 2, d, 0)) % 4
        tz = (z + jnp.where(o == 0, d, 0)) % 4
        return pltpu.make_async_remote_copy(
            src_ref=p3.at[u, f], dst_ref=r3.at[u, d - 1],
            send_sem=gsend.at[u, 2], recv_sem=grecv.at[u, 2],
            device_id=(ty, tx * 8 + tz * 2 + c), device_id_type=MESH,
        )

    def all_of(u, stage):
        buf = (r1, r2, r3)[stage].at[u]
        return pltpu.make_async_remote_copy(
            src_ref=buf, dst_ref=buf, send_sem=gsend.at[u, stage], recv_sem=grecv.at[u, stage],
            device_id=partner, device_id_type=MESH,
        )

    def send_pair(u):
        pair_copy(u).start()

    def step(u, stage):
        if stage == 0:
            pair_copy(u).wait_recv()
            for f in range(4):
                order = ORDERS[order_of(f, u)]
                for i in range(4):
                    for k in range(4):
                        at = {order[0]: i, order[1]: k, order[2]: (f - i - k) % 4}
                        where = (at["y"], at["x"], at["z"])
                        p1[u, f, i, k] = grid[(u, c) + where] + rc[(u,) + where]
        else:
            all_of(u, stage - 1).wait_recv()
            src, got, dst = ((p1, r1, p2), (p2, r2, p3))[stage - 1]
            for f in range(4):
                own = src[u, f, pos[ORDERS[order_of(f, u)][stage - 1]]]
                dst[u, f] = (own + got[u, f, 0]) + (got[u, f, 1] + got[u, f, 2])
        for d in (2, 1, 3):
            if stage == 2:
                last_copy(u, d).start()
            else:
                for f in range(4):
                    axis_copy(u, f, stage, d).start()

    def sum_pair():
        return pltpu.make_async_remote_copy(
            src_ref=s0, dst_ref=sc, send_sem=asend.at[9], recv_sem=arecv.at[9],
            device_id=partner, device_id_type=MESH,
        )

    stages = (("x", sx), ("y", sy), ("z", sz))

    def sum_copy(i, d):
        axis, buf = stages[i]
        return pltpu.make_async_remote_copy(
            src_ref=buf.at[pos[axis]], dst_ref=buf.at[pos[axis]],
            send_sem=asend.at[3 * i + d - 1], recv_sem=arecv.at[3 * i + d - 1],
            device_id=device(axis, d), device_id_type=MESH,
        )

    def sum_step(i):
        if i == 0:
            sum_pair().wait_recv()
            value = s0[...] + sc[...]
        else:
            for d in (1, 2, 3):
                sum_copy(i - 1, d).wait_recv()
            buf = stages[i - 1][1]
            value = (buf[0] + buf[1]) + (buf[2] + buf[3])
        if i < 3:
            axis, buf = stages[i]
            buf[pos[axis]] = value
            for d in (1, 2, 3):
                sum_copy(i, d).start()
        return value

    pl.semaphore_wait(barrier, 10)
    sum_pair().start()

    place(0, da)
    send_pair(0)
    send_pair(1)
    for p in range(1, UNITS // 2):
        buf = (da, db)[p % 2]
        product(p, buf)
        place(p, buf)
        send_pair(2 * p)
        send_pair(2 * p + 1)
        if p == 1:
            sum_step(0)
        step(2 * p - 2, 0)
        step(2 * p - 1, 0)
    for u, stage in (
        (0, 1), (1, 1), (6, 0), (7, 0), (-1, 1), (2, 1), (3, 1), (0, 2), (1, 2), (4, 1), (5, 1),
        (-1, 2), (2, 2), (3, 2), (6, 1), (7, 1), (4, 2), (5, 2), (6, 2), (7, 2),
    ):
        if u < 0:
            sum_step(stage)
        else:
            step(u, stage)
    total = sum_step(3)

    count = total[1]
    mean = total[0] / count
    stats_ref[0] = mean
    stats_ref[1] = count
    index = y * 32 + m
    row = stats_ref[0, pl.ds(index // 16, 1), :]
    lane = lax.broadcasted_iota(jnp.int32, (8, 128), 1)
    sub = lax.broadcasted_iota(jnp.int32, (8, 128), 0)
    picked = jnp.where(lane == (index % 16) * 8 + sub, jnp.broadcast_to(row, (8, 128)), 0.0)
    own_mean = jnp.sum(picked, axis=1, keepdims=True)
    scale = 1.0 / (count - 1.0)
    for u in range(UNITS):
        all_of(u, 2).wait_recv()
        second = (p3[u, own_class] + r3[u, 0]) + (r3[u, 1] + r3[u, 2])
        outer = own_mean * stats_ref[0, u:u + 1, :]
        cov_ref[:, 128 * u:128 * u + 128] = (second - count * outer) / (count - 1.0)

    sum_pair().wait_send()
    for i in range(3):
        for d in (1, 2, 3):
            sum_copy(i, d).wait_send()
    for u in range(UNITS):
        pair_copy(u).wait_send()
        for stage in range(3):
            all_of(u, stage).wait_send()


def finish(stats_ref, cov_ref, count_out, mean_out, cov_out):
    count_out[...] = stats_ref[1, 0:1, 0:1]
    mean_out[...] = stats_ref[0]
    cov_out[...] = cov_ref[...]


def body(features, lengths):
    f32 = jnp.float32
    stats, cov = pl.pallas_call(
        kernel,
        out_shape=(
            jax.ShapeDtypeStruct((2, 8, 128), f32),
            jax.ShapeDtypeStruct((8, D), f32),
        ),
        in_specs=[
            pl.BlockSpec(memory_space=pltpu.HBM),
            pl.BlockSpec(memory_space=pltpu.HBM),
        ],
        out_specs=(
            pl.BlockSpec(memory_space=pltpu.VMEM),
            pl.BlockSpec(memory_space=pltpu.VMEM),
        ),
        scratch_shapes=[
            pltpu.SMEM((1, 2), jnp.int32),
            pltpu.VMEM((ROWS, D), jnp.bfloat16),
            pltpu.VMEM((16, ROWS), jnp.bfloat16),
            pltpu.VMEM((PAIR + 16, D), f32),
            pltpu.VMEM((PAIR, D - PAIR), f32),
            pltpu.VMEM((UNITS, 2, 4, 4, 4, 8, 128), f32),
            pltpu.VMEM((UNITS, 4, 4, 4, 8, 128), f32),
            pltpu.VMEM((UNITS, 4, 4, 8, 128), f32),
            pltpu.VMEM((UNITS, 4, 8, 128), f32),
            pltpu.VMEM((UNITS, 4, 4, 4, 8, 128), f32),
            pltpu.VMEM((UNITS, 4, 3, 4, 8, 128), f32),
            pltpu.VMEM((UNITS, 4, 3, 8, 128), f32),
            pltpu.VMEM((UNITS, 3, 8, 128), f32),
            pltpu.VMEM((2, 8, 128), f32),
            pltpu.VMEM((2, 8, 128), f32),
            pltpu.VMEM((4, 2, 8, 128), f32),
            pltpu.VMEM((4, 2, 8, 128), f32),
            pltpu.VMEM((4, 2, 8, 128), f32),
            pltpu.SemaphoreType.DMA((1,)),
            pltpu.SemaphoreType.DMA((LOADS,)),
            pltpu.SemaphoreType.DMA((UNITS,)),
            pltpu.SemaphoreType.DMA((UNITS,)),
            pltpu.SemaphoreType.DMA((UNITS, 3)),
            pltpu.SemaphoreType.DMA((UNITS, 3)),
            pltpu.SemaphoreType.DMA((10,)),
            pltpu.SemaphoreType.DMA((10,)),
        ],
        compiler_params=pltpu.CompilerParams(
            collective_id=0, has_side_effects=True, vmem_limit_bytes=40 * 1024 * 1024
        ),
        name="gram_reduce",
    )(
        pltpu.with_memory_space_constraint(lengths, pltpu.HBM),
        pltpu.with_memory_space_constraint(features, pltpu.HBM),
    )
    count, mean, cov = pl.pallas_call(
        finish,
        out_shape=(
            jax.ShapeDtypeStruct((1, 1), f32),
            jax.ShapeDtypeStruct((8, 128), f32),
            jax.ShapeDtypeStruct((8, D), f32),
        ),
        in_specs=[pl.BlockSpec(memory_space=pltpu.VMEM)] * 2,
        out_specs=(pl.BlockSpec(memory_space=pltpu.VMEM),) * 3,
        compiler_params=pltpu.CompilerParams(vmem_limit_bytes=1024 * 1024),
        name="finish",
    )(stats, cov)
    return count.reshape(1), mean.reshape(D), cov


def solution(mesh):
    return jax.shard_map(
        body,
        mesh=mesh,
        in_specs=(P(("grp", "mem"), None), P(("grp", "mem"), None)),
        out_specs=(P(), P(), P(("grp", "mem"), None)),
        check_vma=False,
    )
```

```python
import functools

import jax
import jax.numpy as jnp
from jax import lax
from jax.experimental import pallas as pl
from jax.experimental.pallas import tpu as pltpu
from jax.sharding import PartitionSpec as P

MESH = pl.DeviceIdType.MESH
ROWS = 4096
D = 1024
BLK = 128
PAIR = 256
LOADS = ((0, 1024), (1024, 1024), (2048, 1024), (3072, 512), (3584, 512))
UNITS = 8
ORDERS = ("yxz", "xzy", "zyx")


def order_of(f, u):
    return u % 3 if f == 3 else f


def kernel(
    len_hbm, feat, stats_ref, cov_ref,
    len_ref, xb, kt, da, db, grid, p1, p2, p3, rc, r1, r2, r3,
    s0, sc, sx, sy, sz,
    nsem, lsem, csend, crecv, gsend, grecv, asend, arecv,
):
    y = lax.axis_index("grp")
    m = lax.axis_index("mem")
    x, z, c = m // 8, (m // 2) % 4, m % 2
    pos = {"y": y, "x": x, "z": z}

    def device(axis, d):
        at = dict(pos)
        at[axis] = (pos[axis] + d) % 4
        return (at["y"], at["x"] * 8 + at["z"] * 2 + c)

    partner = (y, x * 8 + z * 2 + (1 - c))

    def load(k):
        rows = pl.ds(*LOADS[k])
        return pltpu.make_async_copy(feat.at[rows], xb.at[rows], lsem.at[k])

    lengths_copy = pltpu.make_async_copy(len_hbm, len_ref, nsem.at[0])
    lengths_copy.start()
    for k in range(len(LOADS)):
        load(k).start()

    barrier = pltpu.get_barrier_semaphore()
    pl.semaphore_signal(barrier, inc=1, device_id=partner, device_id_type=MESH)
    for axis in "xyz":
        for d in (1, 2, 3):
            pl.semaphore_signal(barrier, inc=1, device_id=device(axis, d), device_id_type=MESH)

    lengths_copy.wait()

    for k, (start, size) in enumerate(LOADS):
        load(k).wait()
        rows = pl.ds(start, size)
        at = lax.broadcasted_iota(jnp.int32, (16, size), 1) + start % 2048
        keep = (at < len_ref[0, start // 2048]).astype(jnp.float32).astype(jnp.bfloat16)
        kt[:, rows] = keep
        left = xb[rows, 0:PAIR].T * jnp.concatenate([keep] * 16, axis=0)
        prod = jnp.dot(
            jnp.concatenate([left, keep], axis=0), xb[rows, :],
            preferred_element_type=jnp.float32,
        )
        if k == 0:
            da[...] = prod
        else:
            da[...] += prod
    for t in range(8):
        s0[0, t:t + 1, :] = da[PAIR:PAIR + 1, 128 * t:128 * t + 128]
    s0[1] = jnp.full((8, 128), (len_ref[0, 0] + len_ref[0, 1]).astype(jnp.float32))

    def put(u, i, value):
        value = value.reshape(2, 4, 2, 8, 128)
        at = 2 * (i % 2)
        for core in range(2):
            grid[u, core, i // 2, at:at + 2] = value[:, :, core]

    def place(p, dacc):
        for j in (2 * p, 2 * p + 1):
            row = BLK * (j - 2 * p)
            for i in range(j, UNITS):
                col = BLK * (i - 2 * p)
                part = dacc[row:row + BLK, col:col + BLK]
                put(i, j, part)
                if i > j:
                    put(j, i, part.T)

    def product(p, dacc):
        left = xb[:, PAIR * p:PAIR * p + PAIR].T * jnp.concatenate([kt[...]] * 16, axis=0)
        dacc[0:PAIR, 0:D - PAIR * p] = jnp.dot(
            left, xb[:, PAIR * p:], preferred_element_type=jnp.float32
        )

    def pair_copy(u):
        return pltpu.make_async_remote_copy(
            src_ref=grid.at[u, 1 - c], dst_ref=rc.at[u],
            send_sem=csend.at[u], recv_sem=crecv.at[u],
            device_id=partner, device_id_type=MESH,
        )

    own_class = (x + y + z) % 4

    def axis_copy(u, f, stage, d):
        axis = ORDERS[order_of(f, u)][stage]
        to = (pos[axis] + d) % 4
        src = (p1, p2)[stage].at[u, f, to]
        dst = (r1, r2)[stage].at[u, f, d - 1]
        return pltpu.make_async_remote_copy(
            src_ref=src, dst_ref=dst,
            send_sem=gsend.at[u, stage], recv_sem=grecv.at[u, stage],
            device_id=device(axis, d), device_id_type=MESH,
        )

    def last_copy(u, d):
        f = (own_class + d) % 4
        o = jnp.where(f == 3, u % 3, f)
        ty = (y + jnp.where(o == 1, d, 0)) % 4
        tx = (x + jnp.where(o == 2, d, 0)) % 4
        tz = (z + jnp.where(o == 0, d, 0)) % 4
        return pltpu.make_async_remote_copy(
            src_ref=p3.at[u, f], dst_ref=r3.at[u, d - 1],
            send_sem=gsend.at[u, 2], recv_sem=grecv.at[u, 2],
            device_id=(ty, tx * 8 + tz * 2 + c), device_id_type=MESH,
        )

    def all_of(u, stage):
        buf = (r1, r2, r3)[stage].at[u]
        return pltpu.make_async_remote_copy(
            src_ref=buf, dst_ref=buf, send_sem=gsend.at[u, stage], recv_sem=grecv.at[u, stage],
            device_id=partner, device_id_type=MESH,
        )

    def send_pair(u):
        pair_copy(u).start()

    def step(u, stage):
        if stage == 0:
            pair_copy(u).wait_recv()
            for f in range(4):
                order = ORDERS[order_of(f, u)]
                for i in range(4):
                    for k in range(4):
                        at = {order[0]: i, order[1]: k, order[2]: (f - i - k) % 4}
                        where = (at["y"], at["x"], at["z"])
                        p1[u, f, i, k] = grid[(u, c) + where] + rc[(u,) + where]
        else:
            all_of(u, stage - 1).wait_recv()
            src, got, dst = ((p1, r1, p2), (p2, r2, p3))[stage - 1]
            for f in range(4):
                own = src[u, f, pos[ORDERS[order_of(f, u)][stage - 1]]]
                dst[u, f] = (own + got[u, f, 0]) + (got[u, f, 1] + got[u, f, 2])
        for d in (2, 1, 3):
            if stage == 2:
                last_copy(u, d).start()
            else:
                for f in range(4):
                    axis_copy(u, f, stage, d).start()

    def sum_pair():
        return pltpu.make_async_remote_copy(
            src_ref=s0, dst_ref=sc, send_sem=asend.at[9], recv_sem=arecv.at[9],
            device_id=partner, device_id_type=MESH,
        )

    stages = (("x", sx), ("y", sy), ("z", sz))

    def sum_copy(i, d):
        axis, buf = stages[i]
        return pltpu.make_async_remote_copy(
            src_ref=buf.at[pos[axis]], dst_ref=buf.at[pos[axis]],
            send_sem=asend.at[3 * i + d - 1], recv_sem=arecv.at[3 * i + d - 1],
            device_id=device(axis, d), device_id_type=MESH,
        )

    def sum_step(i):
        if i == 0:
            sum_pair().wait_recv()
            value = s0[...] + sc[...]
        else:
            for d in (1, 2, 3):
                sum_copy(i - 1, d).wait_recv()
            buf = stages[i - 1][1]
            value = (buf[0] + buf[1]) + (buf[2] + buf[3])
        if i < 3:
            axis, buf = stages[i]
            buf[pos[axis]] = value
            for d in (1, 2, 3):
                sum_copy(i, d).start()
        return value

    pl.semaphore_wait(barrier, 10)
    sum_pair().start()

    place(0, da)
    send_pair(0)
    send_pair(1)
    for p in range(1, UNITS // 2):
        buf = (da, db)[p % 2]
        product(p, buf)
        place(p, buf)
        send_pair(2 * p)
        send_pair(2 * p + 1)
        if p == 1:
            sum_step(0)
        step(2 * p - 2, 0)
        step(2 * p - 1, 0)
    for u, stage in (
        (0, 1), (1, 1), (6, 0), (7, 0), (-1, 1), (2, 1), (3, 1), (0, 2), (1, 2), (4, 1), (5, 1),
        (-1, 2), (2, 2), (3, 2), (6, 1), (7, 1), (4, 2), (5, 2), (6, 2), (7, 2),
    ):
        if u < 0:
            sum_step(stage)
        else:
            step(u, stage)
    total = sum_step(3)

    count = total[1]
    mean = total[0] / count
    stats_ref[0] = mean
    stats_ref[1] = count
    index = y * 32 + m
    row = stats_ref[0, pl.ds(index // 16, 1), :]
    lane = lax.broadcasted_iota(jnp.int32, (8, 128), 1)
    sub = lax.broadcasted_iota(jnp.int32, (8, 128), 0)
    picked = jnp.where(lane == (index % 16) * 8 + sub, jnp.broadcast_to(row, (8, 128)), 0.0)
    own_mean = jnp.sum(picked, axis=1, keepdims=True)
    for u in range(UNITS):
        all_of(u, 2).wait_recv()
        second = (p3[u, own_class] + r3[u, 0]) + (r3[u, 1] + r3[u, 2])
        outer = own_mean * stats_ref[0, u:u + 1, :]
        cov_ref[:, 128 * u:128 * u + 128] = (second - count * outer) / (count - 1.0)

    sum_pair().wait_send()
    for i in range(3):
        for d in (1, 2, 3):
            sum_copy(i, d).wait_send()
    for u in range(UNITS):
        pair_copy(u).wait_send()
        for stage in range(3):
            all_of(u, stage).wait_send()


def finish(stats_ref, cov_ref, count_out, mean_out, cov_out):
    count_out[...] = stats_ref[1, 0:1, 0:1]
    mean_out[...] = stats_ref[0]
    cov_out[...] = cov_ref[...]


def body(features, lengths):
    f32 = jnp.float32
    stats, cov = pl.pallas_call(
        kernel,
        out_shape=(
            jax.ShapeDtypeStruct((2, 8, 128), f32),
            jax.ShapeDtypeStruct((8, D), f32),
        ),
        in_specs=[
            pl.BlockSpec(memory_space=pltpu.HBM),
            pl.BlockSpec(memory_space=pltpu.HBM),
        ],
        out_specs=(
            pl.BlockSpec(memory_space=pltpu.VMEM),
            pl.BlockSpec(memory_space=pltpu.VMEM),
        ),
        scratch_shapes=[
            pltpu.SMEM((1, 2), jnp.int32),
            pltpu.VMEM((ROWS, D), jnp.bfloat16),
            pltpu.VMEM((16, ROWS), jnp.bfloat16),
            pltpu.VMEM((PAIR + 16, D), f32),
            pltpu.VMEM((PAIR, D - PAIR), f32),
            pltpu.VMEM((UNITS, 2, 4, 4, 4, 8, 128), f32),
            pltpu.VMEM((UNITS, 4, 4, 4, 8, 128), f32),
            pltpu.VMEM((UNITS, 4, 4, 8, 128), f32),
            pltpu.VMEM((UNITS, 4, 8, 128), f32),
            pltpu.VMEM((UNITS, 4, 4, 4, 8, 128), f32),
            pltpu.VMEM((UNITS, 4, 3, 4, 8, 128), f32),
            pltpu.VMEM((UNITS, 4, 3, 8, 128), f32),
            pltpu.VMEM((UNITS, 3, 8, 128), f32),
            pltpu.VMEM((2, 8, 128), f32),
            pltpu.VMEM((2, 8, 128), f32),
            pltpu.VMEM((4, 2, 8, 128), f32),
            pltpu.VMEM((4, 2, 8, 128), f32),
            pltpu.VMEM((4, 2, 8, 128), f32),
            pltpu.SemaphoreType.DMA((1,)),
            pltpu.SemaphoreType.DMA((len(LOADS),)),
            pltpu.SemaphoreType.DMA((UNITS,)),
            pltpu.SemaphoreType.DMA((UNITS,)),
            pltpu.SemaphoreType.DMA((UNITS, 3)),
            pltpu.SemaphoreType.DMA((UNITS, 3)),
            pltpu.SemaphoreType.DMA((10,)),
            pltpu.SemaphoreType.DMA((10,)),
        ],
        compiler_params=pltpu.CompilerParams(
            collective_id=0, has_side_effects=True, vmem_limit_bytes=40 * 1024 * 1024
        ),
        name="gram_reduce",
    )(
        pltpu.with_memory_space_constraint(lengths, pltpu.HBM),
        pltpu.with_memory_space_constraint(features, pltpu.HBM),
    )
    count, mean, cov = pl.pallas_call(
        finish,
        out_shape=(
            jax.ShapeDtypeStruct((1, 1), f32),
            jax.ShapeDtypeStruct((8, 128), f32),
            jax.ShapeDtypeStruct((8, D), f32),
        ),
        in_specs=[pl.BlockSpec(memory_space=pltpu.VMEM)] * 2,
        out_specs=(pl.BlockSpec(memory_space=pltpu.VMEM),) * 3,
        compiler_params=pltpu.CompilerParams(vmem_limit_bytes=1024 * 1024),
        name="finish",
    )(stats, cov)
    return count.reshape(1), mean.reshape(D), cov


def solution(mesh):
    return jax.shard_map(
        body,
        mesh=mesh,
        in_specs=(P(("grp", "mem"), None), P(("grp", "mem"), None)),
        out_specs=(P(), P(), P(("grp", "mem"), None)),
        check_vma=False,
    )
```

```python
import functools

import jax
import jax.numpy as jnp
from jax import lax
from jax.experimental import pallas as pl
from jax.experimental.pallas import tpu as pltpu
from jax.sharding import PartitionSpec as P

MESH = pl.DeviceIdType.MESH
ROWS = 4096
D = 1024
BLK = 128
PAIR = 256
LOADS = ((0, 1024), (1024, 1024), (2048, 1024), (3072, 512), (3584, 512))
UNITS = 8
ORDERS = ("yxz", "xzy", "zyx")


def order_of(f, u):
    return u % 3 if f == 3 else f


def kernel(
    len_hbm, feat, stats_ref, cov_ref,
    len_ref, xb, kt, da, db, grid, p1, p2, p3, rc, r1, r2, r3,
    s0, sc, sx, sy, sz,
    nsem, lsem, csend, crecv, gsend, grecv, asend, arecv,
):
    y = lax.axis_index("grp")
    m = lax.axis_index("mem")
    x, z, c = m // 8, (m // 2) % 4, m % 2
    pos = {"y": y, "x": x, "z": z}

    def device(axis, d):
        at = dict(pos)
        at[axis] = (pos[axis] + d) % 4
        return (at["y"], at["x"] * 8 + at["z"] * 2 + c)

    partner = (y, x * 8 + z * 2 + (1 - c))

    def load(k):
        rows = pl.ds(*LOADS[k])
        return pltpu.make_async_copy(feat.at[rows], xb.at[rows], lsem.at[k])

    lengths_copy = pltpu.make_async_copy(len_hbm, len_ref, nsem.at[0])
    lengths_copy.start()
    for k in range(len(LOADS)):
        load(k).start()

    barrier = pltpu.get_barrier_semaphore()
    pl.semaphore_signal(barrier, inc=1, device_id=partner, device_id_type=MESH)
    for axis in "xyz":
        for d in (1, 2, 3):
            pl.semaphore_signal(barrier, inc=1, device_id=device(axis, d), device_id_type=MESH)

    lengths_copy.wait()

    for k, (start, size) in enumerate(LOADS):
        load(k).wait()
        rows = pl.ds(start, size)
        at = lax.broadcasted_iota(jnp.int32, (16, size), 1) + start % 2048
        keep = (at < len_ref[0, start // 2048]).astype(jnp.float32).astype(jnp.bfloat16)
        kt[:, rows] = keep
        left = xb[rows, 0:PAIR].T * jnp.concatenate([keep] * 16, axis=0)
        prod = jnp.dot(
            jnp.concatenate([left, keep], axis=0), xb[rows, :],
            preferred_element_type=jnp.float32,
        )
        if k == 0:
            da[...] = prod
        else:
            da[...] += prod
    for t in range(8):
        s0[0, t:t + 1, :] = da[PAIR:PAIR + 1, 128 * t:128 * t + 128]
    s0[1] = jnp.full((8, 128), (len_ref[0, 0] + len_ref[0, 1]).astype(jnp.float32))

    def put(u, i, value):
        value = value.reshape(2, 4, 2, 8, 128)
        at = 2 * (i % 2)
        for core in range(2):
            grid[u, core, i // 2, at:at + 2] = value[:, :, core]

    def place(p, dacc):
        for j in (2 * p, 2 * p + 1):
            row = BLK * (j - 2 * p)
            for i in range(j, UNITS):
                col = BLK * (i - 2 * p)
                part = dacc[row:row + BLK, col:col + BLK]
                put(i, j, part)
                if i > j:
                    put(j, i, part.T)

    def product(p, dacc):
        left = xb[:, PAIR * p:PAIR * p + PAIR].T * jnp.concatenate([kt[...]] * 16, axis=0)
        dacc[0:PAIR, 0:D - PAIR * p] = jnp.dot(
            left, xb[:, PAIR * p:], preferred_element_type=jnp.float32
        )

    def pair_copy(u):
        return pltpu.make_async_remote_copy(
            src_ref=grid.at[u, 1 - c], dst_ref=rc.at[u],
            send_sem=csend.at[u], recv_sem=crecv.at[u],
            device_id=partner, device_id_type=MESH,
        )

    own_class = (x + y + z) % 4

    def axis_copy(u, f, stage, d):
        axis = ORDERS[order_of(f, u)][stage]
        to = (pos[axis] + d) % 4
        src = (p1, p2)[stage].at[u, f, to]
        dst = (r1, r2)[stage].at[u, f, d - 1]
        return pltpu.make_async_remote_copy(
            src_ref=src, dst_ref=dst,
            send_sem=gsend.at[u, stage], recv_sem=grecv.at[u, stage],
            device_id=device(axis, d), device_id_type=MESH,
        )

    def last_copy(u, d):
        f = (own_class + d) % 4
        o = jnp.where(f == 3, u % 3, f)
        ty = (y + jnp.where(o == 1, d, 0)) % 4
        tx = (x + jnp.where(o == 2, d, 0)) % 4
        tz = (z + jnp.where(o == 0, d, 0)) % 4
        return pltpu.make_async_remote_copy(
            src_ref=p3.at[u, f], dst_ref=r3.at[u, d - 1],
            send_sem=gsend.at[u, 2], recv_sem=grecv.at[u, 2],
            device_id=(ty, tx * 8 + tz * 2 + c), device_id_type=MESH,
        )

    def all_of(u, stage):
        buf = (r1, r2, r3)[stage].at[u]
        return pltpu.make_async_remote_copy(
            src_ref=buf, dst_ref=buf, send_sem=gsend.at[u, stage], recv_sem=grecv.at[u, stage],
            device_id=partner, device_id_type=MESH,
        )

    def send_pair(u):
        pair_copy(u).start()

    def step(u, stage):
        if stage == 0:
            pair_copy(u).wait_recv()
            for f in range(4):
                order = ORDERS[order_of(f, u)]
                for i in range(4):
                    for k in range(4):
                        at = {order[0]: i, order[1]: k, order[2]: (f - i - k) % 4}
                        where = (at["y"], at["x"], at["z"])
                        p1[u, f, i, k] = grid[(u, c) + where] + rc[(u,) + where]
        else:
            all_of(u, stage - 1).wait_recv()
            src, got, dst = ((p1, r1, p2), (p2, r2, p3))[stage - 1]
            for f in range(4):
                own = src[u, f, pos[ORDERS[order_of(f, u)][stage - 1]]]
                dst[u, f] = (own + got[u, f, 0]) + (got[u, f, 1] + got[u, f, 2])
        for d in (2, 1, 3):
            if stage == 2:
                last_copy(u, d).start()
            else:
                for f in range(4):
                    axis_copy(u, f, stage, d).start()

    def sum_pair():
        return pltpu.make_async_remote_copy(
            src_ref=s0, dst_ref=sc, send_sem=asend.at[9], recv_sem=arecv.at[9],
            device_id=partner, device_id_type=MESH,
        )

    stages = (("x", sx), ("y", sy), ("z", sz))

    def sum_copy(i, d):
        axis, buf = stages[i]
        return pltpu.make_async_remote_copy(
            src_ref=buf.at[pos[axis]], dst_ref=buf.at[pos[axis]],
            send_sem=asend.at[3 * i + d - 1], recv_sem=arecv.at[3 * i + d - 1],
            device_id=device(axis, d), device_id_type=MESH,
        )

    def sum_step(i):
        if i == 0:
            sum_pair().wait_recv()
            value = s0[...] + sc[...]
        else:
            for d in (1, 2, 3):
                sum_copy(i - 1, d).wait_recv()
            buf = stages[i - 1][1]
            value = (buf[0] + buf[1]) + (buf[2] + buf[3])
        if i < 3:
            axis, buf = stages[i]
            buf[pos[axis]] = value
            for d in (1, 2, 3):
                sum_copy(i, d).start()
        return value

    pl.semaphore_wait(barrier, 10)
    sum_pair().start()

    place(0, da)
    send_pair(0)
    send_pair(1)
    for p in range(1, UNITS // 2):
        buf = (da, db)[p % 2]
        product(p, buf)
        place(p, buf)
        send_pair(2 * p)
        send_pair(2 * p + 1)
        if p == 1:
            sum_step(0)
        step(2 * p - 2, 0)
        step(2 * p - 1, 0)
    for u, stage in (
        (0, 1),
        (6, 0),
        (1, 1),
        (7, 0),
        (-1, 1),
        (2, 1),
        (3, 1),
        (4, 1),
        (5, 1),
        (6, 1),
        (7, 1),
        (0, 2),
        (1, 2),
        (-1, 2),
        (2, 2),
        (3, 2),
        (4, 2),
        (5, 2),
        (6, 2),
        (7, 2),
    ):
        if u < 0:
            sum_step(stage)
        else:
            step(u, stage)
    total = sum_step(3)

    count = total[1]
    mean = total[0] / count
    stats_ref[0] = mean
    stats_ref[1] = count
    index = y * 32 + m
    row = stats_ref[0, pl.ds(index // 16, 1), :]
    lane = lax.broadcasted_iota(jnp.int32, (8, 128), 1)
    sub = lax.broadcasted_iota(jnp.int32, (8, 128), 0)
    picked = jnp.where(lane == (index % 16) * 8 + sub, jnp.broadcast_to(row, (8, 128)), 0.0)
    own_mean = jnp.sum(picked, axis=1, keepdims=True)
    for u in range(UNITS):
        all_of(u, 2).wait_recv()
        second = (p3[u, own_class] + r3[u, 0]) + (r3[u, 1] + r3[u, 2])
        outer = own_mean * stats_ref[0, u:u + 1, :]
        cov_ref[:, 128 * u:128 * u + 128] = (second - count * outer) / (count - 1.0)

    sum_pair().wait_send()
    for i in range(3):
        for d in (1, 2, 3):
            sum_copy(i, d).wait_send()
    for u in range(UNITS):
        pair_copy(u).wait_send()
        for stage in range(3):
            all_of(u, stage).wait_send()


def finish(stats_ref, cov_ref, count_out, mean_out, cov_out):
    count_out[...] = stats_ref[1, 0:1, 0:1]
    mean_out[...] = stats_ref[0]
    cov_out[...] = cov_ref[...]


def body(features, lengths):
    f32 = jnp.float32
    stats, cov = pl.pallas_call(
        kernel,
        out_shape=(
            jax.ShapeDtypeStruct((2, 8, 128), f32),
            jax.ShapeDtypeStruct((8, D), f32),
        ),
        in_specs=[
            pl.BlockSpec(memory_space=pltpu.HBM),
            pl.BlockSpec(memory_space=pltpu.HBM),
        ],
        out_specs=(
            pl.BlockSpec(memory_space=pltpu.VMEM),
            pl.BlockSpec(memory_space=pltpu.VMEM),
        ),
        scratch_shapes=[
            pltpu.SMEM((1, 2), jnp.int32),
            pltpu.VMEM((ROWS, D), jnp.bfloat16),
            pltpu.VMEM((16, ROWS), jnp.bfloat16),
            pltpu.VMEM((PAIR + 16, D), f32),
            pltpu.VMEM((PAIR, D - PAIR), f32),
            pltpu.VMEM((UNITS, 2, 4, 4, 4, 8, 128), f32),
            pltpu.VMEM((UNITS, 4, 4, 4, 8, 128), f32),
            pltpu.VMEM((UNITS, 4, 4, 8, 128), f32),
            pltpu.VMEM((UNITS, 4, 8, 128), f32),
            pltpu.VMEM((UNITS, 4, 4, 4, 8, 128), f32),
            pltpu.VMEM((UNITS, 4, 3, 4, 8, 128), f32),
            pltpu.VMEM((UNITS, 4, 3, 8, 128), f32),
            pltpu.VMEM((UNITS, 3, 8, 128), f32),
            pltpu.VMEM((2, 8, 128), f32),
            pltpu.VMEM((2, 8, 128), f32),
            pltpu.VMEM((4, 2, 8, 128), f32),
            pltpu.VMEM((4, 2, 8, 128), f32),
            pltpu.VMEM((4, 2, 8, 128), f32),
            pltpu.SemaphoreType.DMA((1,)),
            pltpu.SemaphoreType.DMA((len(LOADS),)),
            pltpu.SemaphoreType.DMA((UNITS,)),
            pltpu.SemaphoreType.DMA((UNITS,)),
            pltpu.SemaphoreType.DMA((UNITS, 3)),
            pltpu.SemaphoreType.DMA((UNITS, 3)),
            pltpu.SemaphoreType.DMA((10,)),
            pltpu.SemaphoreType.DMA((10,)),
        ],
        compiler_params=pltpu.CompilerParams(
            collective_id=0, has_side_effects=True, vmem_limit_bytes=40 * 1024 * 1024
        ),
        name="gram_reduce",
    )(
        pltpu.with_memory_space_constraint(lengths, pltpu.HBM),
        pltpu.with_memory_space_constraint(features, pltpu.HBM),
    )
    count, mean, cov = pl.pallas_call(
        finish,
        out_shape=(
            jax.ShapeDtypeStruct((1, 1), f32),
            jax.ShapeDtypeStruct((8, 128), f32),
            jax.ShapeDtypeStruct((8, D), f32),
        ),
        in_specs=[pl.BlockSpec(memory_space=pltpu.VMEM)] * 2,
        out_specs=(pl.BlockSpec(memory_space=pltpu.VMEM),) * 3,
        compiler_params=pltpu.CompilerParams(vmem_limit_bytes=1024 * 1024),
        name="finish",
    )(stats, cov)
    return count.reshape(1), mean.reshape(D), cov


def solution(mesh):
    return jax.shard_map(
        body,
        mesh=mesh,
        in_specs=(P(("grp", "mem"), None), P(("grp", "mem"), None)),
        out_specs=(P(), P(), P(("grp", "mem"), None)),
        check_vma=False,
    )
```

```python
import functools

import jax
import jax.numpy as jnp
from jax import lax
from jax.experimental import pallas as pl
from jax.experimental.pallas import tpu as pltpu
from jax.sharding import PartitionSpec as P

MESH = pl.DeviceIdType.MESH
ROWS = 4096
D = 1024
BLK = 128
PAIR = 256
LOADS = ((0, 1024), (1024, 1024), (2048, 1024), (3072, 512), (3584, 512))
UNITS = 8
ORDERS = ("yxz", "xzy", "zyx")


def order_of(f, u):
    return u % 3 if f == 3 else f


def kernel(
    len_hbm, feat, stats_ref, cov_ref,
    len_ref, xb, kt, da, db, grid, p1, p2, p3, rc, r1, r2, r3,
    s0, sc, sx, sy, sz,
    nsem, lsem, csend, crecv, gsend, grecv, asend, arecv,
):
    y = lax.axis_index("grp")
    m = lax.axis_index("mem")
    x, z, c = m // 8, (m // 2) % 4, m % 2
    pos = {"y": y, "x": x, "z": z}

    def device(axis, d):
        at = dict(pos)
        at[axis] = (pos[axis] + d) % 4
        return (at["y"], at["x"] * 8 + at["z"] * 2 + c)

    partner = (y, x * 8 + z * 2 + (1 - c))

    def load(k):
        rows = pl.ds(*LOADS[k])
        return pltpu.make_async_copy(feat.at[rows], xb.at[rows], lsem.at[k])

    lengths_copy = pltpu.make_async_copy(len_hbm, len_ref, nsem.at[0])
    lengths_copy.start()
    for k in range(len(LOADS)):
        load(k).start()

    barrier = pltpu.get_barrier_semaphore()
    pl.semaphore_signal(barrier, inc=1, device_id=partner, device_id_type=MESH)
    for axis in "xyz":
        for d in (1, 2, 3):
            pl.semaphore_signal(barrier, inc=1, device_id=device(axis, d), device_id_type=MESH)

    lengths_copy.wait()

    for k, (start, size) in enumerate(LOADS):
        load(k).wait()
        rows = pl.ds(start, size)
        at = lax.broadcasted_iota(jnp.int32, (16, size), 1) + start % 2048
        keep = (at < len_ref[0, start // 2048]).astype(jnp.float32).astype(jnp.bfloat16)
        kt[:, rows] = keep
        left = xb[rows, 0:PAIR].T * jnp.concatenate([keep] * 16, axis=0)
        prod = jnp.dot(
            jnp.concatenate([left, keep], axis=0), xb[rows, :],
            preferred_element_type=jnp.float32,
        )
        if k == 0:
            da[...] = prod
        else:
            da[...] += prod
    for t in range(8):
        s0[0, t:t + 1, :] = da[PAIR:PAIR + 1, 128 * t:128 * t + 128]
    s0[1] = jnp.full((8, 128), (len_ref[0, 0] + len_ref[0, 1]).astype(jnp.float32))

    def put(u, i, value):
        value = value.reshape(2, 4, 2, 8, 128)
        at = 2 * (i % 2)
        for core in range(2):
            grid[u, core, i // 2, at:at + 2] = value[:, :, core]

    def place(p, dacc):
        for j in (2 * p, 2 * p + 1):
            row = BLK * (j - 2 * p)
            for i in range(j, UNITS):
                col = BLK * (i - 2 * p)
                part = dacc[row:row + BLK, col:col + BLK]
                put(i, j, part)
                if i > j:
                    put(j, i, part.T)

    def product(p, dacc):
        left = xb[:, PAIR * p:PAIR * p + PAIR].T * jnp.concatenate([kt[...]] * 16, axis=0)
        dacc[0:PAIR, 0:D - PAIR * p] = jnp.dot(
            left, xb[:, PAIR * p:], preferred_element_type=jnp.float32
        )

    def pair_copy(u):
        return pltpu.make_async_remote_copy(
            src_ref=grid.at[u, 1 - c], dst_ref=rc.at[u],
            send_sem=csend.at[u], recv_sem=crecv.at[u],
            device_id=partner, device_id_type=MESH,
        )

    own_class = (x + y + z) % 4

    def axis_copy(u, f, stage, d):
        axis = ORDERS[order_of(f, u)][stage]
        to = (pos[axis] + d) % 4
        src = (p1, p2)[stage].at[u, f, to]
        dst = (r1, r2)[stage].at[u, f, d - 1]
        return pltpu.make_async_remote_copy(
            src_ref=src, dst_ref=dst,
            send_sem=gsend.at[u, stage], recv_sem=grecv.at[u, stage],
            device_id=device(axis, d), device_id_type=MESH,
        )

    def last_copy(u, d):
        f = (own_class + d) % 4
        o = jnp.where(f == 3, u % 3, f)
        ty = (y + jnp.where(o == 1, d, 0)) % 4
        tx = (x + jnp.where(o == 2, d, 0)) % 4
        tz = (z + jnp.where(o == 0, d, 0)) % 4
        return pltpu.make_async_remote_copy(
            src_ref=p3.at[u, f], dst_ref=r3.at[u, d - 1],
            send_sem=gsend.at[u, 2], recv_sem=grecv.at[u, 2],
            device_id=(ty, tx * 8 + tz * 2 + c), device_id_type=MESH,
        )

    def all_of(u, stage):
        buf = (r1, r2, r3)[stage].at[u]
        return pltpu.make_async_remote_copy(
            src_ref=buf, dst_ref=buf, send_sem=gsend.at[u, stage], recv_sem=grecv.at[u, stage],
            device_id=partner, device_id_type=MESH,
        )

    def send_pair(u):
        pair_copy(u).start()

    def step(u, stage):
        if stage == 0:
            pair_copy(u).wait_recv()
            for f in range(4):
                order = ORDERS[order_of(f, u)]
                for i in range(4):
                    for k in range(4):
                        at = {order[0]: i, order[1]: k, order[2]: (f - i - k) % 4}
                        where = (at["y"], at["x"], at["z"])
                        p1[u, f, i, k] = grid[(u, c) + where] + rc[(u,) + where]
        else:
            all_of(u, stage - 1).wait_recv()
            src, got, dst = ((p1, r1, p2), (p2, r2, p3))[stage - 1]
            for f in range(4):
                own = src[u, f, pos[ORDERS[order_of(f, u)][stage - 1]]]
                dst[u, f] = (own + got[u, f, 0]) + (got[u, f, 1] + got[u, f, 2])
        for d in (2, 1, 3):
            if stage == 2:
                last_copy(u, d).start()
            else:
                for f in range(4):
                    axis_copy(u, f, stage, d).start()

    def sum_pair():
        return pltpu.make_async_remote_copy(
            src_ref=s0, dst_ref=sc, send_sem=asend.at[9], recv_sem=arecv.at[9],
            device_id=partner, device_id_type=MESH,
        )

    stages = (("x", sx), ("y", sy), ("z", sz))

    def sum_copy(i, d):
        axis, buf = stages[i]
        return pltpu.make_async_remote_copy(
            src_ref=buf.at[pos[axis]], dst_ref=buf.at[pos[axis]],
            send_sem=asend.at[3 * i + d - 1], recv_sem=arecv.at[3 * i + d - 1],
            device_id=device(axis, d), device_id_type=MESH,
        )

    def sum_step(i):
        if i == 0:
            sum_pair().wait_recv()
            value = s0[...] + sc[...]
        else:
            for d in (1, 2, 3):
                sum_copy(i - 1, d).wait_recv()
            buf = stages[i - 1][1]
            value = (buf[0] + buf[1]) + (buf[2] + buf[3])
        if i < 3:
            axis, buf = stages[i]
            buf[pos[axis]] = value
            for d in (1, 2, 3):
                sum_copy(i, d).start()
        return value

    pl.semaphore_wait(barrier, 10)
    sum_pair().start()

    place(0, da)
    send_pair(0)
    send_pair(1)
    for p in range(1, UNITS // 2):
        buf = (da, db)[p % 2]
        product(p, buf)
        place(p, buf)
        send_pair(2 * p)
        send_pair(2 * p + 1)
        if p == 1:
            sum_step(0)
        step(2 * p - 2, 0)
        step(2 * p - 1, 0)
    for u, stage in (
        (6, 0),
        (7, 0),
        (0, 1),
        (1, 1),
        (2, 1),
        (3, 1),
        (-1, 1),
        (4, 1),
        (5, 1),
        (6, 1),
        (7, 1),
        (-1, 2),
        (0, 2),
        (1, 2),
        (2, 2),
        (3, 2),
        (4, 2),
        (5, 2),
        (6, 2),
        (7, 2),
    ):
        if u < 0:
            sum_step(stage)
        else:
            step(u, stage)
    total = sum_step(3)

    count = total[1]
    mean = total[0] / count
    stats_ref[0] = mean
    stats_ref[1] = count
    index = y * 32 + m
    row = stats_ref[0, pl.ds(index // 16, 1), :]
    lane = lax.broadcasted_iota(jnp.int32, (8, 128), 1)
    sub = lax.broadcasted_iota(jnp.int32, (8, 128), 0)
    picked = jnp.where(lane == (index % 16) * 8 + sub, jnp.broadcast_to(row, (8, 128)), 0.0)
    own_mean = jnp.sum(picked, axis=1, keepdims=True)
    for u in range(UNITS):
        all_of(u, 2).wait_recv()
        second = (p3[u, own_class] + r3[u, 0]) + (r3[u, 1] + r3[u, 2])
        outer = own_mean * stats_ref[0, u:u + 1, :]
        cov_ref[:, 128 * u:128 * u + 128] = (second - count * outer) / (count - 1.0)

    sum_pair().wait_send()
    for i in range(3):
        for d in (1, 2, 3):
            sum_copy(i, d).wait_send()
    for u in range(UNITS):
        pair_copy(u).wait_send()
        for stage in range(3):
            all_of(u, stage).wait_send()


def finish(stats_ref, cov_ref, count_out, mean_out, cov_out):
    count_out[...] = stats_ref[1, 0:1, 0:1]
    mean_out[...] = stats_ref[0]
    cov_out[...] = cov_ref[...]


def body(features, lengths):
    f32 = jnp.float32
    stats, cov = pl.pallas_call(
        kernel,
        out_shape=(
            jax.ShapeDtypeStruct((2, 8, 128), f32),
            jax.ShapeDtypeStruct((8, D), f32),
        ),
        in_specs=[
            pl.BlockSpec(memory_space=pltpu.HBM),
            pl.BlockSpec(memory_space=pltpu.HBM),
        ],
        out_specs=(
            pl.BlockSpec(memory_space=pltpu.VMEM),
            pl.BlockSpec(memory_space=pltpu.VMEM),
        ),
        scratch_shapes=[
            pltpu.SMEM((1, 2), jnp.int32),
            pltpu.VMEM((ROWS, D), jnp.bfloat16),
            pltpu.VMEM((16, ROWS), jnp.bfloat16),
            pltpu.VMEM((PAIR + 16, D), f32),
            pltpu.VMEM((PAIR, D - PAIR), f32),
            pltpu.VMEM((UNITS, 2, 4, 4, 4, 8, 128), f32),
            pltpu.VMEM((UNITS, 4, 4, 4, 8, 128), f32),
            pltpu.VMEM((UNITS, 4, 4, 8, 128), f32),
            pltpu.VMEM((UNITS, 4, 8, 128), f32),
            pltpu.VMEM((UNITS, 4, 4, 4, 8, 128), f32),
            pltpu.VMEM((UNITS, 4, 3, 4, 8, 128), f32),
            pltpu.VMEM((UNITS, 4, 3, 8, 128), f32),
            pltpu.VMEM((UNITS, 3, 8, 128), f32),
            pltpu.VMEM((2, 8, 128), f32),
            pltpu.VMEM((2, 8, 128), f32),
            pltpu.VMEM((4, 2, 8, 128), f32),
            pltpu.VMEM((4, 2, 8, 128), f32),
            pltpu.VMEM((4, 2, 8, 128), f32),
            pltpu.SemaphoreType.DMA((1,)),
            pltpu.SemaphoreType.DMA((len(LOADS),)),
            pltpu.SemaphoreType.DMA((UNITS,)),
            pltpu.SemaphoreType.DMA((UNITS,)),
            pltpu.SemaphoreType.DMA((UNITS, 3)),
            pltpu.SemaphoreType.DMA((UNITS, 3)),
            pltpu.SemaphoreType.DMA((10,)),
            pltpu.SemaphoreType.DMA((10,)),
        ],
        compiler_params=pltpu.CompilerParams(
            collective_id=0, has_side_effects=True, vmem_limit_bytes=40 * 1024 * 1024
        ),
        name="gram_reduce",
    )(
        pltpu.with_memory_space_constraint(lengths, pltpu.HBM),
        pltpu.with_memory_space_constraint(features, pltpu.HBM),
    )
    count, mean, cov = pl.pallas_call(
        finish,
        out_shape=(
            jax.ShapeDtypeStruct((1, 1), f32),
            jax.ShapeDtypeStruct((8, 128), f32),
            jax.ShapeDtypeStruct((8, D), f32),
        ),
        in_specs=[pl.BlockSpec(memory_space=pltpu.VMEM)] * 2,
        out_specs=(pl.BlockSpec(memory_space=pltpu.VMEM),) * 3,
        compiler_params=pltpu.CompilerParams(vmem_limit_bytes=1024 * 1024),
        name="finish",
    )(stats, cov)
    return count.reshape(1), mean.reshape(D), cov


def solution(mesh):
    return jax.shard_map(
        body,
        mesh=mesh,
        in_specs=(P(("grp", "mem"), None), P(("grp", "mem"), None)),
        out_specs=(P(), P(), P(("grp", "mem"), None)),
        check_vma=False,
    )
```
